1024 devices in a mesh: loop: 64 (over z_lo, x, core), tensor: 16 (over y, z_hi).
Axes of the slice: x: 8, y: 8, z: 8 (z_hi: 2, z_lo: 4; z = z_hi * 4 + z_lo), core: 2. Of those that a mesh axis runs over, the one named last changes fastest.
Arguments:
- grad_out: bfloat16 [8192, 4096], P('loop', 'tensor'), may hold values from -6 to 6
- saved_hidden: bfloat16 [1664, 32768], P('tensor', 'loop'), may hold values from -6 to 6
- picked_tokens: int32 [2, 1664], replicated, may hold values from 0 to 8191, as said below
- gate_values: float32 [2, 1664], replicated, may hold values from 0.25 to 1
- in_weight: bfloat16 [4096, 32768], P(None, 'loop'), may hold values from -0.09375 to 0.09375
- out_weight: bfloat16 [32768, 4096], P('loop'), may hold values from -0.046875 to 0.046875
Outputs:
- input_grad: bfloat16 [8192, 4096], P('loop', 'tensor')
The draws below stay inside these ranges and needn't reach their ends.
Inputs may be any that keep to these rules, and one draw needn't show every extreme that they name: Each row picked_tokens[e] lists 1664 distinct token indices in ascending order; among the 128 tokens of one loop index (an aligned block) it names at most 28, and in every row some block holds exactly 28.
All inputs are finite; a program needn't handle non-finite values.
Results may differ from the reference program's by a relative error of at most 0.0032.
Values may be sent and summed in bfloat16 or wider, within the bound.
A program may use at most 32 MiB of HBM per device.

```python
import math
import jax
import jax.numpy as jnp

D = 4096
FF = 16384
EXPERTS = 2
PB = 26
SWING = 2
TOK_LOOP = 128
CAP = 1664
TOKENS = 8192


def shuffle_block(block_key):
    return jax.random.permutation(block_key, TOK_LOOP)


def draw_picked_tokens(key, part):
    block_total = TOKENS // TOK_LOOP
    expert_keys = jax.random.split(jax.random.fold_in(key, 7), EXPERTS)

    def one_expert(subkey):
        quota_key, order_key = jax.random.split(subkey)
        shuffled = jax.random.permutation(quota_key, block_total)
        pair_count = block_total // 4
        raised = shuffled[0:2 * pair_count:2]
        lowered = shuffled[1:2 * pair_count:2]
        quotas = jnp.full((block_total,), PB, jnp.int32).at[raised].add(SWING).at[lowered].add(-SWING)
        order_keys = jax.random.split(order_key, block_total)
        shuffles = jax.vmap(shuffle_block)(order_keys)
        ranking = jnp.argsort(shuffles, axis=1).astype(jnp.int32)
        chosen = ranking < quotas[:, None]
        return jnp.nonzero(chosen.reshape(-1), size=CAP)[0].astype(jnp.int32)
    return jax.vmap(one_expert)(expert_keys)


def block_levels(stream_key, shape, cuts, smallest, largest):
    gain = 1.0
    for axis_at, blocks in cuts:
        draws = jax.random.uniform(jax.random.fold_in(jax.random.fold_in(stream_key, 6), axis_at), (blocks,), jnp.float32, smallest / len(cuts), largest / len(cuts))
        gain = gain * jnp.repeat(jnp.exp(draws), shape[axis_at] // blocks).reshape((-1,) + (1,) * (len(shape) - 1 - axis_at))
    return gain


def noise(stream_key, dims, spread, reach, cuts=(), kind=jnp.bfloat16):
    values = jax.random.normal(stream_key, dims, jnp.float32) * spread
    if len(cuts) > 0:
        values = block_levels(stream_key, dims, cuts, -0.22, 0.18) * values
    return jnp.clip(values, min=-reach, max=reach).astype(kind)


def setup_inputs(seed: int = 0) -> dict:
    keys = jax.random.split(jax.random.key(seed), 7)
    grad_out = noise(keys[0], (TOKENS, D), 1.0, 6.0, ((0, 64), (1, 16)))
    saved_hidden = noise(keys[1], (CAP, EXPERTS * FF), 1.5, 6.0, ((0, 16), (1, 64)))
    picked_tokens = draw_picked_tokens(jax.random.fold_in(keys[6], 71), 0)
    gate_values = jnp.clip(jax.random.uniform(keys[3], (EXPERTS, CAP), jnp.float32, 0.25, 1.0), 0.25, 1.0)
    in_weight = noise(keys[4], (D, EXPERTS * FF), D ** -0.5, 0.09375, ((1, 64),))
    out_weight = noise(keys[5], (EXPERTS * FF, D), FF ** -0.5, 0.046875, ((0, 64),))
    return {"grad_out": grad_out, "saved_hidden": saved_hidden, "picked_tokens": picked_tokens, "gate_values": gate_values, "in_weight": in_weight, "out_weight": out_weight}


slope_scale = math.sqrt(2.0 / math.pi)

def gelu_slope(values):
    inner = slope_scale * (values + 0.044715 * values * values * values)
    bent = jnp.tanh(inner)
    return 0.5 * (1.0 + bent) + 0.5 * values * (1.0 - bent * bent) * slope_scale * (1.0 + 0.134145 * values * values)

def reference(grad_out, saved_hidden, picked_tokens, gate_values, in_weight, out_weight):
    moe_grad = jnp.zeros((TOKENS, D), jnp.float32)
    for expert in range(EXPERTS):
        chosen = picked_tokens[expert]
        scaled = (gate_values[expert][:, None] * grad_out[chosen].astype(jnp.float32)).astype(jnp.bfloat16)
        out_block = out_weight[expert * FF:(expert + 1) * FF]
        act_grad = jnp.dot(scaled, out_block.T, preferred_element_type=jnp.float32)
        hidden_block = saved_hidden[:, expert * FF:(expert + 1) * FF].astype(jnp.float32)
        pre_grad = (act_grad * gelu_slope(hidden_block)).astype(jnp.bfloat16)
        in_block = in_weight[:, expert * FF:(expert + 1) * FF]
        partial_grad = jnp.dot(pre_grad, in_block.T, preferred_element_type=jnp.float32)
        moe_grad = moe_grad.at[chosen].add(partial_grad)
    return (grad_out.astype(jnp.float32) + moe_grad).astype(jnp.bfloat16)
```

```python
import functools
import math

import jax
import jax.numpy as jnp
from jax import lax
from jax.experimental import pallas as pl
from jax.experimental.pallas import tpu as pltpu
from jax.sharding import PartitionSpec as P

MOST = 28
SLOTS = 32
CORES = 2
PLANES = 2
CHUNKS = 3
MESH = pl.DeviceIdType.MESH

slope_scale = math.sqrt(2.0 / math.pi)


def gelu_slope(values):
    inner = slope_scale * (values + 0.044715 * values * values * values)
    bent = jnp.tanh(inner)
    return 0.5 * (1.0 + bent) + 0.5 * values * (1.0 - bent * bent) * slope_scale * (
        1.0 + 0.134145 * values * values
    )


def window_size(blocks, capacity, chunks):
    rows = capacity // chunks
    spare = MOST * blocks - capacity
    widest = 0
    for chunk in range(chunks):
        low = rows * chunk // MOST
        high = max(b for b in range(blocks) if max(0, MOST * b - spare) < rows * (chunk + 1))
        widest = max(widest, high - low + 1)
    return widest


def by_distance(ring):
    order = []
    for d in range(1, ring // 2 + 1):
        order.append(d)
        if ring - d != d:
            order.append(ring - d)
    return order


def dot_nt(a, b):
    return lax.dot_general(a, b, (((1,), (1,)), ((), ())), preferred_element_type=jnp.float32)


def dot_tn(a, b):
    return lax.dot_general(a, b, (((0,), (0,)), ((), ())), preferred_element_type=jnp.float32)


def dot_nn(a, b):
    return lax.dot_general(a, b, (((1,), (0,)), ((), ())), preferred_element_type=jnp.float32)


def split_exact(values):
    high = values.astype(jnp.bfloat16)
    low = (values - high.astype(jnp.float32)).astype(jnp.bfloat16)
    return high, low


def kernel(
    sizes,
    grad_ref,
    hidden_ref,
    picks_ref,
    gates_ref,
    chunk_ref,
    in_hbm,
    out_hbm,
    result_ref,
    in_ref,
    out_ref,
    slot_ref,
    arrive_ref,
    wide_ref,
    core_send,
    core_recv,
    plane_send,
    plane_recv,
    own_ref,
    ring_send,
    ring_recv,
    back_ref,
    home_ref,
    weight_sem,
    a_send,
    a_recv,
    bx_send,
    bx_recv,
    bz_send,
    bz_recv,
    bc_send,
    bc_recv,
    cc_send,
    cc_recv,
    cz_send,
    cz_recv,
    cx_send,
    cx_recv,
    d_send,
    d_recv,
):
    experts, chunks, blocks, ring, window = sizes
    block_rows, home_cols = grad_ref.shape
    rows, width = hidden_ref.shape
    features = in_ref.shape[0]
    capacity = picks_ref.shape[1]
    group = blocks // experts
    piece = features // group
    halves = group // chunks
    quarter = features // (CORES * PLANES)
    f32, bf16, i32 = jnp.float32, jnp.bfloat16, jnp.int32

    loop, chunk = lax.axis_index("loop"), lax.axis_index("tensor")
    expert = loop // group
    place = lax.rem(loop, group)
    plane = place // (ring * CORES)
    spot = lax.rem(place // CORES, ring)
    core = lax.rem(place, CORES)
    slice_id = core * (PLANES * ring) + plane * ring + spot
    slice_home = slice_id // halves
    slice_half = lax.rem(slice_id, halves)

    def start_of(t):
        return jnp.minimum(rows * t // MOST, blocks - window)

    def first_of(b):
        return (MOST * jnp.maximum(b - window + 1, 0) + rows - 1) // rows

    def loop_of(e, p, s, c):
        return e * group + (p * ring + s) * CORES + c

    def loop_of_slice(e, j):
        return loop_of(e, lax.rem(j // ring, PLANES), lax.rem(j, ring), j // (PLANES * ring))

    first = first_of(loop)
    begin = start_of(chunk)

    def at_slice(c, p, s):
        return pl.ds(pl.multiple_of((c * (PLANES * ring) + p * ring + s) * piece, piece), piece)

    def targets(body):
        for k in range(CHUNKS):
            t = first + k

            @pl.when((t < chunks) & (start_of(t) <= loop))
            def _():
                for e in range(experts):
                    for h in range(halves):
                        body(e, k, h, loop_of_slice(e, chunk * halves + h), t)

    weights = (
        pltpu.make_async_copy(out_hbm, out_ref, weight_sem.at[0]),
        pltpu.make_async_copy(in_hbm, in_ref, weight_sem.at[1]),
    )
    for copy in weights:
        copy.start()
    home_ref[...] = jnp.zeros_like(home_ref)

    barrier = pltpu.get_barrier_semaphore()

    def greet(l, t):
        pl.semaphore_signal(barrier, inc=1, device_id=(l, t), device_id_type=MESH)

    def greet_other(l, t):
        @pl.when((l != loop) | (t != chunk))
        def _():
            greet(l, t)

    targets(lambda e, k, h, l, t: greet_other(l, t))
    for i in range(window):
        greet_other(begin + i, slice_home)
    for d in range(1, ring):
        greet(loop_of(expert, plane, lax.rem(spot + d, ring), core), chunk)
    greet(loop_of(expert, 1 - plane, spot, core), chunk)
    greet(loop_of(expert, plane, spot, 1 - core), chunk)

    tokens = loop * block_rows + lax.broadcasted_iota(i32, (block_rows, 1), 0)
    grad = grad_ref[...].astype(f32)
    below = (
        lax.broadcasted_iota(i32, (block_rows, block_rows), 1)
        < lax.broadcasted_iota(i32, (block_rows, block_rows), 0)
    ).astype(f32).astype(bf16)
    slot_lane = lax.broadcasted_iota(i32, (block_rows, SLOTS), 1)
    spread = []
    for e in range(experts):
        same = picks_ref[e : e + 1, :] == tokens
        picked = jnp.sum(jnp.where(same, 1.0, 0.0), axis=1, keepdims=True)
        gate = jnp.sum(jnp.where(same, gates_ref[e : e + 1, :], 0.0), axis=1, keepdims=True)
        wide_picked = jnp.broadcast_to(picked, (block_rows, SLOTS))
        rank = dot_nn(below, wide_picked.astype(bf16)).astype(i32)
        one_hot = jnp.where(
            (rank == slot_lane) & (wide_picked > 0.5), 1.0, 0.0
        ).astype(bf16)
        spread.append(one_hot)
        scaled = (gate * grad).astype(bf16)
        slots = dot_tn(one_hot, scaled).astype(bf16)
        for h in range(halves):
            slot_ref[e, h] = slots[:, h * piece : (h + 1) * piece]

    window_lines = 16 * ((window + 15) // 16)
    block_line = begin + lax.broadcasted_iota(i32, (window_lines, 1), 0)
    earlier = picks_ref[pl.ds(expert, 1), :] < block_line * block_rows
    first_pick = jnp.sum(jnp.where(earlier, 1.0, 0.0), axis=1, keepdims=True).astype(i32)
    block_of = chunk_ref[pl.ds(expert * chunks + chunk, 1), :] // block_rows
    first_row = jnp.sum(
        jnp.where(block_of == block_line, first_pick, 0), axis=0, keepdims=True
    )
    place_of = (
        (block_of - begin) * SLOTS
        + chunk * rows
        + lax.broadcasted_iota(i32, (1, rows), 1)
        - first_row
    )
    select = jnp.where(
        lax.broadcasted_iota(i32, (window * SLOTS, rows), 0) == place_of, 1.0, 0.0
    ).astype(bf16)

    greeted = (
        jnp.where(first + 1 < chunks, jnp.where(start_of(first + 1) <= loop, 1, 0), 0)
        + jnp.where(first + 2 < chunks, jnp.where(start_of(first + 2) <= loop, 1, 0), 0)
        + 1
    )
    own_window = (
        (slice_home == chunk) & (begin <= loop) & (loop < begin + window)
    )
    pl.semaphore_wait(
        barrier,
        greeted * (experts * halves) + window + (ring - 1) + 2 - jnp.where(own_window, 2, 0),
    )

    def a_copy(e, k, h, l, t):
        return pltpu.make_async_remote_copy(
            src_ref=slot_ref.at[e, h],
            dst_ref=arrive_ref.at[loop - start_of(t)],
            send_sem=a_send.at[e, k, h],
            recv_sem=a_recv,
            device_id=(l, t),
            device_id_type=MESH,
        )

    def a_start(e, k, h, l, t):
        @pl.when((l != loop) | (t != chunk))
        def _():
            a_copy(e, k, h, l, t).start()

        @pl.when((l == loop) & (t == chunk))
        def _():
            pltpu.make_async_copy(
                slot_ref.at[e, h], arrive_ref.at[loop - start_of(t)], a_recv
            ).start()

    def a_finish(e, k, h, l, t):
        @pl.when((l != loop) | (t != chunk))
        def _():
            a_copy(e, k, h, l, t).wait_send()

    targets(a_start)
    slope = gelu_slope(hidden_ref[...].astype(f32))
    pltpu.make_async_copy(arrive_ref, arrive_ref, a_recv).wait()
    mine = dot_tn(select, arrive_ref[...].reshape(window * SLOTS, piece)).astype(bf16)
    wide_ref[:, at_slice(core, plane, spot)] = mine

    order = by_distance(ring)

    def bx_copy(d):
        here = wide_ref.at[:, at_slice(core, plane, spot)]
        return pltpu.make_async_remote_copy(
            src_ref=here,
            dst_ref=here,
            send_sem=bx_send.at[d],
            recv_sem=bx_recv.at[d],
            device_id=(loop_of(expert, plane, lax.rem(spot + d, ring), core), chunk),
            device_id_type=MESH,
        )

    def bz_copy(d):
        here = wide_ref.at[:, at_slice(core, plane, lax.rem(spot + ring - d, ring))]
        return pltpu.make_async_remote_copy(
            src_ref=here,
            dst_ref=here,
            send_sem=bz_send.at[d],
            recv_sem=bz_recv.at[d],
            device_id=(loop_of(expert, 1 - plane, spot, core), chunk),
            device_id_type=MESH,
        )

    def bc_copy(p, d):
        other = plane if p == 0 else 1 - plane
        here = wide_ref.at[:, at_slice(core, other, lax.rem(spot + ring - d, ring))]
        return pltpu.make_async_remote_copy(
            src_ref=here,
            dst_ref=here,
            send_sem=bc_send.at[p, d],
            recv_sem=bc_recv.at[p, d],
            device_id=(loop_of(expert, plane, spot, 1 - core), chunk),
            device_id_type=MESH,
        )

    def quarter_of(c, p):
        return pl.ds(pl.multiple_of((c * PLANES + p) * quarter, quarter), quarter)

    def first_product(c, p):
        here = quarter_of(c, p)
        return dot_nt(wide_ref[:, here], out_ref[:, here])

    for d in order:
        bx_copy(d).start()
    bz_copy(0).start()
    bc_copy(0, 0).start()
    for d in order:
        bx_copy(d).wait_recv()
        bz_copy(d).start()
        bc_copy(0, d).start()
    weights[0].wait()
    act = first_product(core, plane)
    for d in [0] + order:
        bz_copy(d).wait_recv()
        bc_copy(1, d).start()
    act += first_product(core, 1 - plane)
    for d in [0] + order:
        bc_copy(0, d).wait_recv()
    act += first_product(1 - core, plane)
    for d in [0] + order:
        bc_copy(1, d).wait_recv()
    act += first_product(1 - core, 1 - plane)
    pre = (act * slope).astype(bf16)

    def second_product(c, p):
        return dot_nt(pre, in_ref[quarter_of(c, p), :])

    def cc_copy(p):
        return pltpu.make_async_remote_copy(
            src_ref=core_send.at[p],
            dst_ref=core_recv.at[p],
            send_sem=cc_send.at[p],
            recv_sem=cc_recv.at[p],
            device_id=(loop_of(expert, plane, spot, 1 - core), chunk),
            device_id_type=MESH,
        )

    def at_spot(s):
        return pl.ds(pl.multiple_of(s * piece, piece), piece)

    def cz_copy(d):
        here = at_spot(lax.rem(spot + d, ring))
        return pltpu.make_async_remote_copy(
            src_ref=plane_send.at[:, here],
            dst_ref=plane_recv.at[:, here],
            send_sem=cz_send.at[d],
            recv_sem=cz_recv.at[d],
            device_id=(loop_of(expert, 1 - plane, spot, core), chunk),
            device_id_type=MESH,
        )

    def cx_copy(d):
        return pltpu.make_async_remote_copy(
            src_ref=ring_send.at[d],
            dst_ref=ring_recv.at[d],
            send_sem=cx_send.at[d],
            recv_sem=cx_recv.at[d],
            device_id=(loop_of(expert, plane, lax.rem(spot + d, ring), core), chunk),
            device_id_type=MESH,
        )

    far_first = list(reversed(order))
    weights[1].wait()
    core_send[1] = second_product(1 - core, 1 - plane).astype(core_send.dtype)
    cc_copy(1).start()
    core_send[0] = second_product(1 - core, plane).astype(core_send.dtype)
    cc_copy(0).start()
    partial = second_product(core, 1 - plane)
    cc_copy(1).wait_recv()
    plane_send[...] = (partial + core_recv[1].astype(f32)).astype(bf16)
    for d in far_first + [0]:
        cz_copy(d).start()
    partial = second_product(core, plane)
    cc_copy(0).wait_recv()
    own_ref[...] = partial + core_recv[0].astype(f32)
    for d in far_first:
        cz_copy(d).wait_recv()
        here = at_spot(lax.rem(spot + d, ring))
        ring_send[d] = (own_ref[:, here] + plane_recv[:, here].astype(f32)).astype(bf16)
        cx_copy(d).start()
    cz_copy(0).wait_recv()
    total = own_ref[:, at_spot(spot)] + plane_recv[:, at_spot(spot)].astype(f32)
    for d in order:
        cx_copy(d).wait_recv()
        total += ring_recv[d].astype(f32)

    high, low = split_exact(total)
    back = dot_nn(select, high) + dot_nn(select, low)
    back_ref[...] = back.reshape(window, SLOTS, piece).astype(back_ref.dtype)

    def d_copy(i):
        home = begin + i
        k = chunk - first_of(home)
        return pltpu.make_async_remote_copy(
            src_ref=back_ref.at[i],
            dst_ref=home_ref.at[expert, k, slice_half],
            send_sem=d_send.at[i],
            recv_sem=d_recv.at[expert, k, slice_half],
            device_id=(home, slice_home),
            device_id_type=MESH,
        )

    def d_start(i):
        home = begin + i

        @pl.when((home != loop) | (slice_home != chunk))
        def _():
            d_copy(i).start()

        @pl.when((home == loop) & (slice_home == chunk))
        def _():
            k = chunk - first_of(home)
            pltpu.make_async_copy(
                back_ref.at[i],
                home_ref.at[expert, k, slice_half],
                d_recv.at[expert, k, slice_half],
            ).start()

    for i in range(window):
        d_start(i)

    targets(a_finish)
    for d in order:
        bx_copy(d).wait_send()
        cx_copy(d).wait_send()
    for d in [0] + order:
        bz_copy(d).wait_send()
        cz_copy(d).wait_send()
        for p in range(PLANES):
            bc_copy(p, d).wait_send()
    for p in range(PLANES):
        cc_copy(p).wait_send()

    def d_wait(e, k, h, l, t):
        pltpu.make_async_copy(
            home_ref.at[e, k, h], home_ref.at[e, k, h], d_recv.at[e, k, h]
        ).wait()

    targets(d_wait)
    moe = jnp.zeros((block_rows, home_cols), f32)
    for e in range(experts):
        parts = []
        for h in range(halves):
            part = home_ref[e, 0, h].astype(f32)
            for k in range(1, CHUNKS):
                part += home_ref[e, k, h].astype(f32)
            parts.append(part)
        high, low = split_exact(jnp.concatenate(parts, axis=1))
        moe += dot_nn(spread[e], high) + dot_nn(spread[e], low)
    result_ref[...] = (grad_ref[...].astype(f32) + moe).astype(result_ref.dtype)
    for i in range(window):
        home = begin + i

        @pl.when((home != loop) | (slice_home != chunk))
        def _():
            d_copy(i).wait_send()


def shards(ring, grad_out, saved_hidden, picked_tokens, gate_values, in_weight, out_weight):
    blocks, chunks = lax.axis_size("loop"), lax.axis_size("tensor")
    experts, capacity = picked_tokens.shape
    rows, width = saved_hidden.shape[0], in_weight.shape[1]
    features = in_weight.shape[0]
    window = window_size(blocks, capacity, chunks)
    group = blocks // experts
    piece = features // group
    halves = group // chunks
    quarter = features // (CORES * PLANES)
    bf16, f32 = jnp.bfloat16, jnp.float32
    vmem, dma = pltpu.VMEM, pltpu.SemaphoreType.DMA
    in_vmem = pl.BlockSpec(memory_space=pltpu.VMEM)
    in_hbm = pl.BlockSpec(memory_space=pl.ANY)
    return pl.pallas_call(
        functools.partial(kernel, (experts, chunks, blocks, ring, window)),
        out_shape=jax.ShapeDtypeStruct(grad_out.shape, bf16),
        in_specs=[in_vmem] * 5 + [in_hbm] * 2,
        out_specs=in_vmem,
        scratch_shapes=[
            vmem((features, width), bf16),
            vmem((width, features), bf16),
            vmem((experts, halves, SLOTS, piece), bf16),
            vmem((window, SLOTS, piece), bf16),
            vmem((rows, features), bf16),
            vmem((PLANES, rows, quarter), bf16),
            vmem((PLANES, rows, quarter), bf16),
            vmem((rows, quarter), bf16),
            vmem((rows, quarter), bf16),
            vmem((rows, quarter), f32),
            vmem((ring, rows, piece), bf16),
            vmem((ring, rows, piece), bf16),
            vmem((window, SLOTS, piece), f32),
            vmem((experts, CHUNKS, halves, SLOTS, piece), f32),
            dma((2,)),
            dma((experts, CHUNKS, halves)),
            dma,
            dma((ring,)),
            dma((ring,)),
            dma((ring,)),
            dma((ring,)),
            dma((PLANES, ring)),
            dma((PLANES, ring)),
            dma((PLANES,)),
            dma((PLANES,)),
            dma((ring,)),
            dma((ring,)),
            dma((ring,)),
            dma((ring,)),
            dma((window,)),
            dma((experts, CHUNKS, halves)),
        ],
        compiler_params=pltpu.CompilerParams(collective_id=0, has_side_effects=True),
    )(
        grad_out,
        saved_hidden,
        picked_tokens,
        gate_values,
        picked_tokens.reshape(experts * chunks, rows),
        in_weight,
        out_weight,
    )


def solution(mesh):
    ring = mesh.shape["loop"] // (2 * PLANES * CORES)
    placed = (
        P("loop", "tensor"),
        P("tensor", "loop"),
        P(),
        P(),
        P(None, "loop"),
        P("loop", None),
    )
    return jax.shard_map(
        functools.partial(shards, ring),
        mesh=mesh,
        in_specs=placed,
        out_specs=P("loop", "tensor"),
        check_vma=False,
    )
```

```python
import functools
import math

import jax
import jax.numpy as jnp
from jax import lax
from jax.experimental import pallas as pl
from jax.experimental.pallas import tpu as pltpu
from jax.sharding import PartitionSpec as P

MOST = 28
SLOTS = 32
LANES = 128
CORES = 2
PLANES = 2
CHUNKS = 3
MESH = pl.DeviceIdType.MESH

slope_scale = math.sqrt(2.0 / math.pi)


def gelu_slope(values):
    inner = slope_scale * (values + 0.044715 * values * values * values)
    bent = jnp.tanh(inner)
    return 0.5 * (1.0 + bent) + 0.5 * values * (1.0 - bent * bent) * slope_scale * (
        1.0 + 0.134145 * values * values
    )


def window_size(blocks, capacity, chunks):
    rows = capacity // chunks
    spare = MOST * blocks - capacity
    widest = 0
    for chunk in range(chunks):
        low = rows * chunk // MOST
        high = max(b for b in range(blocks) if max(0, MOST * b - spare) < rows * (chunk + 1))
        widest = max(widest, high - low + 1)
    return widest


def by_distance(ring):
    order = []
    for d in range(1, ring // 2 + 1):
        order.append(d)
        if ring - d != d:
            order.append(ring - d)
    return order


def dot_nt(a, b):
    return lax.dot_general(a, b, (((1,), (1,)), ((), ())), preferred_element_type=jnp.float32)


def dot_tn(a, b):
    return lax.dot_general(a, b, (((0,), (0,)), ((), ())), preferred_element_type=jnp.float32)


def dot_nn(a, b):
    return lax.dot_general(a, b, (((1,), (0,)), ((), ())), preferred_element_type=jnp.float32)


def kernel(
    sizes,
    grad_hbm,
    hidden_hbm,
    picks_hbm,
    gates_hbm,
    in_hbm,
    out_hbm,
    result_ref,
    grad_ref,
    hidden_ref,
    picks_ref,
    gates_ref,
    in_ref,
    out_ref,
    slot_ref,
    arrive_ref,
    wide_ref,
    core_send,
    core_recv,
    plane_send,
    plane_recv,
    own_ref,
    ring_send,
    ring_recv,
    back_ref,
    home_ref,
    input_sem,
    weight_sem,
    a_send,
    a_recv,
    bx_send,
    bx_recv,
    bz_send,
    bz_recv,
    bc_send,
    bc_recv,
    cc_send,
    cc_recv,
    cz_send,
    cz_recv,
    cx_send,
    cx_recv,
    d_send,
    d_recv,
):
    experts, chunks, blocks, ring, window = sizes
    block_rows, home_cols = grad_hbm.shape
    rows, width = hidden_hbm.shape
    features = in_hbm.shape[0]
    capacity = picks_hbm.shape[1]
    group = blocks // experts
    piece = features // group
    halves = group // chunks
    quarter = features // (CORES * PLANES)
    f32, bf16, i32 = jnp.float32, jnp.bfloat16, jnp.int32

    loop, chunk = lax.axis_index("loop"), lax.axis_index("tensor")
    expert = loop // group
    place = lax.rem(loop, group)
    plane = place // (ring * CORES)
    spot = lax.rem(place // CORES, ring)
    core = lax.rem(place, CORES)
    def start_of(t):
        return jnp.minimum(rows * t // MOST, blocks - window)

    def first_of(b):
        return (MOST * jnp.maximum(b - window + 1, 0) + rows - 1) // rows

    def loop_of(e, p, s, c):
        return e * group + (p * ring + s) * CORES + c

    def middle(t):
        return start_of(t) + window // 2

    def near_plane(e, t):
        return jnp.clip(middle(t) // (ring * CORES) - e * PLANES, 0, PLANES - 1)

    def turn(e, t):
        return middle(t) // CORES + (experts - 1 - e) * (ring // 2)

    def spot_of_home(e, t, home):
        return lax.rem(turn(e, t) + 3 * (t // PLANES + ring - home // PLANES), ring)

    def plane_of_home(e, t, home):
        near = near_plane(e, t)
        return jnp.where(lax.rem(home, PLANES) == lax.rem(t, PLANES), near, 1 - near)

    def home_of(e, t, p, s):
        side = lax.rem(t, PLANES)
        lane = lax.rem(t // PLANES + 3 * (turn(e, t) + ring - s), ring)
        return lane * PLANES + jnp.where(p == near_plane(e, t), side, 1 - side)

    first = first_of(loop)
    begin = start_of(chunk)
    slice_home = home_of(expert, chunk, plane, spot)
    slice_half = core

    def at_slice(c, p, s):
        return pl.ds(pl.multiple_of((c * (PLANES * ring) + p * ring + s) * piece, piece), piece)

    def targets(body):
        for k in range(CHUNKS):
            t = first + k

            @pl.when((t < chunks) & (start_of(t) <= loop))
            def _():
                for e in range(experts):
                    for h in range(halves):
                        p, s = plane_of_home(e, t, chunk), spot_of_home(e, t, chunk)
                        body(e, k, h, loop_of(e, p, s, h), t)

    home_ref[...] = jnp.zeros_like(home_ref)
    arrive_ref[...] = jnp.zeros_like(arrive_ref)
    used = pl.ds(0, MOST)

    barrier = pltpu.get_barrier_semaphore()

    def greet(l, t):
        pl.semaphore_signal(barrier, inc=1, device_id=(l, t), device_id_type=MESH)

    def greet_other(l, t):
        @pl.when((l != loop) | (t != chunk))
        def _():
            greet(l, t)

    targets(lambda e, k, h, l, t: greet_other(l, t))
    for i in range(window):
        greet_other(begin + i, slice_home)
    for d in range(1, ring):
        greet(loop_of(expert, plane, lax.rem(spot + d, ring), core), chunk)
    greet(loop_of(expert, 1 - plane, spot, core), chunk)
    greet(loop_of(expert, plane, spot, 1 - core), chunk)

    inputs = [
        pltpu.make_async_copy(here, there, input_sem.at[i])
        for i, (here, there) in enumerate(
            (
                (picks_hbm, picks_ref),
                (gates_hbm, gates_ref),
                (grad_hbm, grad_ref),
                (hidden_hbm, hidden_ref),
            )
        )
    ]
    for copy in inputs:
        copy.start()

    for copy in inputs:
        copy.wait()
    tokens = loop * block_rows + lax.broadcasted_iota(i32, (block_rows, 1), 0)
    grad = grad_ref[...].astype(f32)
    below = (
        lax.broadcasted_iota(i32, (block_rows, block_rows), 1)
        < lax.broadcasted_iota(i32, (block_rows, block_rows), 0)
    ).astype(f32).astype(bf16)
    slot_lane = lax.broadcasted_iota(i32, (block_rows, SLOTS), 1)
    spread = []
    for e in range(experts):
        same = picks_ref[e : e + 1, :] == tokens
        picked = jnp.sum(jnp.where(same, 1.0, 0.0), axis=1, keepdims=True)
        gate = jnp.sum(jnp.where(same, gates_ref[e : e + 1, :], 0.0), axis=1, keepdims=True)
        wide_picked = jnp.broadcast_to(picked, (block_rows, SLOTS))
        rank = dot_nn(below, wide_picked.astype(bf16)).astype(i32)
        one_hot = jnp.where(
            (rank == slot_lane) & (wide_picked > 0.5), 1.0, 0.0
        ).astype(bf16)
        spread.append(one_hot)
        scaled = (gate * grad).astype(bf16)
        slots = dot_tn(one_hot, scaled).astype(bf16)
        for h in range(halves):
            slot_ref[e, h] = slots[:, h * piece : (h + 1) * piece]

    window_lines = 16 * ((window + 15) // 16)
    block_line = begin + lax.broadcasted_iota(i32, (window_lines, 1), 0)
    earlier = picks_ref[pl.ds(expert, 1), :] < block_line * block_rows
    first_pick = jnp.sum(jnp.where(earlier, 1.0, 0.0), axis=1, keepdims=True).astype(i32)
    tile = chunk * rows // LANES
    shift = chunk * rows - tile * LANES
    last = capacity // LANES - 1
    lane = lax.broadcasted_iota(i32, (8, LANES), 1)

    def picks_tile(i):
        here = pl.ds(pl.multiple_of(jnp.minimum(i, last) * LANES, LANES), LANES)
        row = picks_ref[0:1, here]
        for e in range(1, experts):
            row = jnp.where(expert == e, picks_ref[e : e + 1, here], row)
        wide = jnp.broadcast_to(row, (8, LANES))
        return pltpu.roll(wide, lax.rem(LANES - shift, LANES), 1)

    own_picks = jnp.where(lane < LANES - shift, picks_tile(tile), picks_tile(tile + 1))
    block_of = own_picks[0:1, 0:rows] // block_rows
    first_row = jnp.sum(
        jnp.where(block_of == block_line, first_pick, 0), axis=0, keepdims=True
    )
    place_of = (
        (block_of - begin) * SLOTS
        + chunk * rows
        + lax.broadcasted_iota(i32, (1, rows), 1)
        - first_row
    )
    select = jnp.where(
        lax.broadcasted_iota(i32, (window * SLOTS, rows), 0) == place_of, 1.0, 0.0
    ).astype(bf16)

    slope = gelu_slope(hidden_ref[...].astype(f32))
    greeted = (
        jnp.where(first + 1 < chunks, jnp.where(start_of(first + 1) <= loop, 1, 0), 0)
        + jnp.where(first + 2 < chunks, jnp.where(start_of(first + 2) <= loop, 1, 0), 0)
        + 1
    )
    own_window = (
        (slice_home == chunk) & (begin <= loop) & (loop < begin + window)
    )
    pl.semaphore_wait(
        barrier,
        greeted * (experts * halves) + window + (ring - 1) + 2 - jnp.where(own_window, 2, 0),
    )

    def a_copy(e, k, h, l, t):
        return pltpu.make_async_remote_copy(
            src_ref=slot_ref.at[e, h, used],
            dst_ref=arrive_ref.at[loop - start_of(t), used],
            send_sem=a_send.at[e, k, h],
            recv_sem=a_recv,
            device_id=(l, t),
            device_id_type=MESH,
        )

    def a_start(e, k, h, l, t):
        @pl.when((l != loop) | (t != chunk))
        def _():
            a_copy(e, k, h, l, t).start()

        @pl.when((l == loop) & (t == chunk))
        def _():
            pltpu.make_async_copy(
                slot_ref.at[e, h, used], arrive_ref.at[loop - start_of(t), used], a_recv
            ).start()

    def a_finish(e, k, h, l, t):
        @pl.when((l != loop) | (t != chunk))
        def _():
            a_copy(e, k, h, l, t).wait_send()

    targets(a_start)

    for c in range(CORES):
        for p in range(PLANES):
            for s in range(ring):
                t = home_of(expert, chunk, p, s)
                source = pl.ds(pl.multiple_of((t * CORES + c) * piece, piece), piece)
                target = pl.ds((c * (PLANES * ring) + p * ring + s) * piece, piece)
                pltpu.make_async_copy(
                    out_hbm.at[:, source], out_ref.at[:, target], weight_sem.at[0]
                ).start()
                pltpu.make_async_copy(
                    in_hbm.at[source, :], in_ref.at[target, :], weight_sem.at[1]
                ).start()
    weights = (
        pltpu.make_async_copy(out_ref, out_ref, weight_sem.at[0]),
        pltpu.make_async_copy(in_ref, in_ref, weight_sem.at[1]),
    )
    everything = arrive_ref.at[:, used]
    pltpu.make_async_copy(everything, everything, a_recv).wait()
    mine = dot_tn(select, arrive_ref[...].reshape(window * SLOTS, piece)).astype(bf16)
    wide_ref[:, at_slice(core, plane, spot)] = mine

    order = by_distance(ring)

    def bx_copy(d):
        here = wide_ref.at[:, at_slice(core, plane, spot)]
        return pltpu.make_async_remote_copy(
            src_ref=here,
            dst_ref=here,
            send_sem=bx_send.at[d],
            recv_sem=bx_recv.at[d],
            device_id=(loop_of(expert, plane, lax.rem(spot + d, ring), core), chunk),
            device_id_type=MESH,
        )

    def bz_copy(d):
        here = wide_ref.at[:, at_slice(core, plane, lax.rem(spot + ring - d, ring))]
        return pltpu.make_async_remote_copy(
            src_ref=here,
            dst_ref=here,
            send_sem=bz_send.at[d],
            recv_sem=bz_recv.at[d],
            device_id=(loop_of(expert, 1 - plane, spot, core), chunk),
            device_id_type=MESH,
        )

    def bc_copy(p, d):
        other = plane if p == 0 else 1 - plane
        here = wide_ref.at[:, at_slice(core, other, lax.rem(spot + ring - d, ring))]
        return pltpu.make_async_remote_copy(
            src_ref=here,
            dst_ref=here,
            send_sem=bc_send.at[p, d],
            recv_sem=bc_recv.at[p, d],
            device_id=(loop_of(expert, plane, spot, 1 - core), chunk),
            device_id_type=MESH,
        )

    def quarter_of(c, p):
        return pl.ds(pl.multiple_of((c * PLANES + p) * quarter, quarter), quarter)

    def first_product(c, p):
        here = quarter_of(c, p)
        return dot_nt(wide_ref[:, here], out_ref[:, here])

    for d in order:
        bx_copy(d).start()
    bz_copy(0).start()
    bc_copy(0, 0).start()
    for d in order:
        bx_copy(d).wait_recv()
        bz_copy(d).start()
        bc_copy(0, d).start()
    weights[0].wait()
    act = first_product(core, plane)
    for d in [0] + order:
        bz_copy(d).wait_recv()
        bc_copy(1, d).start()
    act += first_product(core, 1 - plane)
    for d in [0] + order:
        bc_copy(0, d).wait_recv()
    act += first_product(1 - core, plane)
    for d in [0] + order:
        bc_copy(1, d).wait_recv()
    act += first_product(1 - core, 1 - plane)
    pre = (act * slope).astype(bf16)

    def second_product(c, p):
        return dot_nt(pre, in_ref[quarter_of(c, p), :])

    def cc_copy(p):
        return pltpu.make_async_remote_copy(
            src_ref=core_send.at[p],
            dst_ref=core_recv.at[p],
            send_sem=cc_send.at[p],
            recv_sem=cc_recv.at[p],
            device_id=(loop_of(expert, plane, spot, 1 - core), chunk),
            device_id_type=MESH,
        )

    def at_spot(s):
        return pl.ds(pl.multiple_of(s * piece, piece), piece)

    def cz_copy(d):
        here = at_spot(lax.rem(spot + d, ring))
        return pltpu.make_async_remote_copy(
            src_ref=plane_send.at[:, here],
            dst_ref=plane_recv.at[:, here],
            send_sem=cz_send.at[d],
            recv_sem=cz_recv.at[d],
            device_id=(loop_of(expert, 1 - plane, spot, core), chunk),
            device_id_type=MESH,
        )

    def cx_copy(d):
        return pltpu.make_async_remote_copy(
            src_ref=ring_send.at[d],
            dst_ref=ring_recv.at[d],
            send_sem=cx_send.at[d],
            recv_sem=cx_recv.at[d],
            device_id=(loop_of(expert, plane, lax.rem(spot + d, ring), core), chunk),
            device_id_type=MESH,
        )

    far_first = list(reversed(order))
    weights[1].wait()
    core_send[1] = second_product(1 - core, 1 - plane).astype(core_send.dtype)
    cc_copy(1).start()
    core_send[0] = second_product(1 - core, plane).astype(core_send.dtype)
    cc_copy(0).start()
    partial = second_product(core, 1 - plane)
    cc_copy(1).wait_recv()
    plane_send[...] = (partial + core_recv[1].astype(f32)).astype(bf16)
    for d in far_first + [0]:
        cz_copy(d).start()
    partial = second_product(core, plane)
    cc_copy(0).wait_recv()
    own_ref[...] = partial + core_recv[0].astype(f32)
    for d in far_first:
        cz_copy(d).wait_recv()
        here = at_spot(lax.rem(spot + d, ring))
        ring_send[d] = (own_ref[:, here] + plane_recv[:, here].astype(f32)).astype(bf16)
        cx_copy(d).start()
    cz_copy(0).wait_recv()
    total = own_ref[:, at_spot(spot)] + plane_recv[:, at_spot(spot)].astype(f32)
    for d in order:
        cx_copy(d).wait_recv()
        total += ring_recv[d].astype(f32)

    back = dot_nn(select, total.astype(bf16)).astype(bf16)
    back_ref[...] = back.reshape(window, SLOTS, piece)

    def d_copy(i):
        home = begin + i
        k = chunk - first_of(home)
        return pltpu.make_async_remote_copy(
            src_ref=back_ref.at[i, used],
            dst_ref=home_ref.at[expert, k, slice_half, used],
            send_sem=d_send.at[i],
            recv_sem=d_recv.at[expert, k, slice_half],
            device_id=(home, slice_home),
            device_id_type=MESH,
        )

    def d_start(i):
        home = begin + i

        @pl.when((home != loop) | (slice_home != chunk))
        def _():
            d_copy(i).start()

        @pl.when((home == loop) & (slice_home == chunk))
        def _():
            k = chunk - first_of(home)
            pltpu.make_async_copy(
                back_ref.at[i, used],
                home_ref.at[expert, k, slice_half, used],
                d_recv.at[expert, k, slice_half],
            ).start()

    for i in range(window):
        d_start(i)

    targets(a_finish)
    for d in order:
        bx_copy(d).wait_send()
        cx_copy(d).wait_send()
    for d in [0] + order:
        bz_copy(d).wait_send()
        cz_copy(d).wait_send()
        for p in range(PLANES):
            bc_copy(p, d).wait_send()
    for p in range(PLANES):
        cc_copy(p).wait_send()

    def d_wait(e, k, h, l, t):
        pltpu.make_async_copy(
            home_ref.at[e, k, h, used], home_ref.at[e, k, h, used], d_recv.at[e, k, h]
        ).wait()

    targets(d_wait)
    moe = jnp.zeros((block_rows, home_cols), f32)
    for e in range(experts):
        parts = []
        for h in range(halves):
            part = home_ref[e, 0, h].astype(f32)
            for k in range(1, CHUNKS):
                part += home_ref[e, k, h].astype(f32)
            parts.append(part)
        moe += dot_nn(spread[e], jnp.concatenate(parts, axis=1).astype(bf16))
    result_ref[...] = (grad_ref[...].astype(f32) + moe).astype(result_ref.dtype)
    for i in range(window):
        home = begin + i

        @pl.when((home != loop) | (slice_home != chunk))
        def _():
            d_copy(i).wait_send()


def shards(ring, grad_out, saved_hidden, picked_tokens, gate_values, in_weight, out_weight):
    blocks, chunks = lax.axis_size("loop"), lax.axis_size("tensor")
    experts, capacity = picked_tokens.shape
    rows, width = saved_hidden.shape[0], in_weight.shape[1]
    features = in_weight.shape[0]
    window = window_size(blocks, capacity, chunks)
    group = blocks // experts
    piece = features // group
    halves = group // chunks
    quarter = features // (CORES * PLANES)
    bf16, f32 = jnp.bfloat16, jnp.float32
    vmem, dma = pltpu.VMEM, pltpu.SemaphoreType.DMA
    in_vmem = pl.BlockSpec(memory_space=pltpu.VMEM)
    in_hbm = pl.BlockSpec(memory_space=pl.ANY)
    return pl.pallas_call(
        functools.partial(kernel, (experts, chunks, blocks, ring, window)),
        out_shape=jax.ShapeDtypeStruct(grad_out.shape, bf16),
        in_specs=[in_hbm] * 6,
        out_specs=in_vmem,
        scratch_shapes=[
            vmem(grad_out.shape, bf16),
            vmem(saved_hidden.shape, bf16),
            vmem(picked_tokens.shape, jnp.int32),
            vmem(gate_values.shape, f32),
            vmem((features, width), bf16),
            vmem((width, features), bf16),
            vmem((experts, halves, SLOTS, piece), bf16),
            vmem((window, SLOTS, piece), bf16),
            vmem((rows, features), bf16),
            vmem((PLANES, rows, quarter), bf16),
            vmem((PLANES, rows, quarter), bf16),
            vmem((rows, quarter), bf16),
            vmem((rows, quarter), bf16),
            vmem((rows, quarter), f32),
            vmem((ring, rows, piece), bf16),
            vmem((ring, rows, piece), bf16),
            vmem((window, SLOTS, piece), bf16),
            vmem((experts, CHUNKS, halves, SLOTS, piece), bf16),
            dma((4,)),
            dma((2,)),
            dma((experts, CHUNKS, halves)),
            dma,
            dma((ring,)),
            dma((ring,)),
            dma((ring,)),
            dma((ring,)),
            dma((PLANES, ring)),
            dma((PLANES, ring)),
            dma((PLANES,)),
            dma((PLANES,)),
            dma((ring,)),
            dma((ring,)),
            dma((ring,)),
            dma((ring,)),
            dma((window,)),
            dma((experts, CHUNKS, halves)),
        ],
        compiler_params=pltpu.CompilerParams(collective_id=0, has_side_effects=True),
    )(
        grad_out,
        saved_hidden,
        picked_tokens,
        gate_values,
        in_weight,
        out_weight,
    )


def solution(mesh):
    ring = mesh.shape["loop"] // (2 * PLANES * CORES)
    placed = (
        P("loop", "tensor"),
        P("tensor", "loop"),
        P(),
        P(),
        P(None, "loop"),
        P("loop", None),
    )
    return jax.shard_map(
        functools.partial(shards, ring),
        mesh=mesh,
        in_specs=placed,
        out_specs=P("loop", "tensor"),
        check_vma=False,
    )
```

```python
import functools
import math

import jax
import jax.numpy as jnp
from jax import lax
from jax.experimental import pallas as pl
from jax.experimental.pallas import tpu as pltpu
from jax.sharding import PartitionSpec as P

MOST = 28
SLOTS = 32
LANES = 128
CORES = 2
PLANES = 2
CHUNKS = 3
MESH = pl.DeviceIdType.MESH

slope_scale = math.sqrt(2.0 / math.pi)


def gelu_slope(values):
    inner = slope_scale * (values + 0.044715 * values * values * values)
    bent = jnp.tanh(inner)
    return 0.5 * (1.0 + bent) + 0.5 * values * (1.0 - bent * bent) * slope_scale * (
        1.0 + 0.134145 * values * values
    )


def window_size(blocks, capacity, chunks):
    rows = capacity // chunks
    spare = MOST * blocks - capacity
    widest = 0
    for chunk in range(chunks):
        low = rows * chunk // MOST
        high = max(b for b in range(blocks) if max(0, MOST * b - spare) < rows * (chunk + 1))
        widest = max(widest, high - low + 1)
    return widest


def by_distance(ring):
    order = []
    for d in range(1, ring // 2 + 1):
        order.append(d)
        if ring - d != d:
            order.append(ring - d)
    return order


def dot_nt(a, b):
    return lax.dot_general(a, b, (((1,), (1,)), ((), ())), preferred_element_type=jnp.float32)


def dot_tn(a, b):
    return lax.dot_general(a, b, (((0,), (0,)), ((), ())), preferred_element_type=jnp.float32)


def dot_nn(a, b):
    return lax.dot_general(a, b, (((1,), (0,)), ((), ())), preferred_element_type=jnp.float32)


def kernel(
    sizes,
    grad_hbm,
    hidden_hbm,
    picks_hbm,
    gates_hbm,
    in_hbm,
    out_hbm,
    result_ref,
    grad_ref,
    hidden_ref,
    picks_ref,
    gates_ref,
    in_ref,
    out_ref,
    slot_ref,
    arrive_ref,
    wide_ref,
    core_send,
    core_recv,
    plane_send,
    plane_recv,
    own_ref,
    side_recv,
    last_send,
    ring_send,
    ring_recv,
    back_ref,
    home_ref,
    input_sem,
    weight_sem,
    a_send,
    a_recv,
    bx_send,
    bx_recv,
    bz_send,
    bz_recv,
    bc_send,
    bc_recv,
    cc_send,
    cc_recv,
    cz_send,
    cz_recv,
    cx_send,
    cx_recv,
    cs_send,
    cs_recv,
    d_send,
    d_recv,
):
    experts, chunks, blocks, ring, window = sizes
    block_rows, home_cols = grad_hbm.shape
    rows, width = hidden_hbm.shape
    features = in_hbm.shape[0]
    capacity = picks_hbm.shape[1]
    group = blocks // experts
    piece = features // group
    halves = group // chunks
    quarter = features // (CORES * PLANES)
    f32, bf16, i32 = jnp.float32, jnp.bfloat16, jnp.int32

    loop, chunk = lax.axis_index("loop"), lax.axis_index("tensor")
    expert = loop // group
    place = lax.rem(loop, group)
    plane = place // (ring * CORES)
    spot = lax.rem(place // CORES, ring)
    core = lax.rem(place, CORES)
    def start_of(t):
        return jnp.minimum(rows * t // MOST, blocks - window)

    def first_of(b):
        return (MOST * jnp.maximum(b - window + 1, 0) + rows - 1) // rows

    def loop_of(e, p, s, c):
        return e * group + (p * ring + s) * CORES + c

    def middle(t):
        return start_of(t) + window // 2

    def near_plane(e, t):
        return jnp.clip(middle(t) // (ring * CORES) - e * PLANES, 0, PLANES - 1)

    def turn(e, t):
        return middle(t) // CORES + (experts - 1 - e) * (ring // 2)

    def spot_of_home(e, t, home):
        return lax.rem(turn(e, t) + 3 * (t // PLANES + ring - home // PLANES), ring)

    def plane_of_home(e, t, home):
        near = near_plane(e, t)
        return jnp.where(lax.rem(home, PLANES) == lax.rem(t, PLANES), near, 1 - near)

    def home_of(e, t, p, s):
        side = lax.rem(t, PLANES)
        lane = lax.rem(t // PLANES + 3 * (turn(e, t) + ring - s), ring)
        return lane * PLANES + jnp.where(p == near_plane(e, t), side, 1 - side)

    first = first_of(loop)
    begin = start_of(chunk)
    slice_home = home_of(expert, chunk, plane, spot)
    slice_half = core

    def at_slice(c, p, s):
        return pl.ds(pl.multiple_of((c * (PLANES * ring) + p * ring + s) * piece, piece), piece)

    def targets(body):
        for k in range(CHUNKS):
            t = first + k

            @pl.when((t < chunks) & (start_of(t) <= loop))
            def _():
                for e in range(experts):
                    for h in range(halves):
                        p, s = plane_of_home(e, t, chunk), spot_of_home(e, t, chunk)
                        body(e, k, h, loop_of(e, p, s, h), t)

    home_ref[...] = jnp.zeros_like(home_ref)
    arrive_ref[...] = jnp.zeros_like(arrive_ref)
    used = pl.ds(0, MOST)

    barrier = pltpu.get_barrier_semaphore()

    def greet(l, t):
        pl.semaphore_signal(barrier, inc=1, device_id=(l, t), device_id_type=MESH)

    def greet_other(l, t):
        @pl.when((l != loop) | (t != chunk))
        def _():
            greet(l, t)

    targets(lambda e, k, h, l, t: greet_other(l, t))
    for i in range(window):
        greet_other(begin + i, slice_home)
    for d in range(1, ring):
        greet(loop_of(expert, plane, lax.rem(spot + d, ring), core), chunk)
    greet(loop_of(expert, 1 - plane, spot, core), chunk)
    greet(loop_of(expert, plane, spot, 1 - core), chunk)

    inputs = [
        pltpu.make_async_copy(here, there, input_sem.at[i])
        for i, (here, there) in enumerate(
            (
                (picks_hbm, picks_ref),
                (gates_hbm, gates_ref),
                (grad_hbm, grad_ref),
                (hidden_hbm, hidden_ref),
            )
        )
    ]
    for copy in inputs:
        copy.start()

    for copy in inputs:
        copy.wait()
    tokens = loop * block_rows + lax.broadcasted_iota(i32, (block_rows, 1), 0)
    grad = grad_ref[...].astype(f32)
    below = (
        lax.broadcasted_iota(i32, (block_rows, block_rows), 1)
        < lax.broadcasted_iota(i32, (block_rows, block_rows), 0)
    ).astype(f32).astype(bf16)
    slot_lane = lax.broadcasted_iota(i32, (block_rows, SLOTS), 1)
    spread = []
    for e in range(experts):
        same = picks_ref[e : e + 1, :] == tokens
        picked = jnp.sum(jnp.where(same, 1.0, 0.0), axis=1, keepdims=True)
        gate = jnp.sum(jnp.where(same, gates_ref[e : e + 1, :], 0.0), axis=1, keepdims=True)
        wide_picked = jnp.broadcast_to(picked, (block_rows, SLOTS))
        rank = dot_nn(below, wide_picked.astype(bf16)).astype(i32)
        one_hot = jnp.where(
            (rank == slot_lane) & (wide_picked > 0.5), 1.0, 0.0
        ).astype(bf16)
        spread.append(one_hot)
        scaled = (gate * grad).astype(bf16)
        slots = dot_tn(one_hot, scaled).astype(bf16)
        for h in range(halves):
            slot_ref[e, h] = slots[:, h * piece : (h + 1) * piece]

    window_lines = 16 * ((window + 15) // 16)
    block_line = begin + lax.broadcasted_iota(i32, (window_lines, 1), 0)
    earlier = picks_ref[pl.ds(expert, 1), :] < block_line * block_rows
    first_pick = jnp.sum(jnp.where(earlier, 1.0, 0.0), axis=1, keepdims=True).astype(i32)
    tile = chunk * rows // LANES
    shift = chunk * rows - tile * LANES
    last = capacity // LANES - 1
    lane = lax.broadcasted_iota(i32, (8, LANES), 1)

    def picks_tile(i):
        here = pl.ds(pl.multiple_of(jnp.minimum(i, last) * LANES, LANES), LANES)
        row = picks_ref[0:1, here]
        for e in range(1, experts):
            row = jnp.where(expert == e, picks_ref[e : e + 1, here], row)
        wide = jnp.broadcast_to(row, (8, LANES))
        return pltpu.roll(wide, lax.rem(LANES - shift, LANES), 1)

    own_picks = jnp.where(lane < LANES - shift, picks_tile(tile), picks_tile(tile + 1))
    block_of = own_picks[0:1, 0:rows] // block_rows
    first_row = jnp.sum(
        jnp.where(block_of == block_line, first_pick, 0), axis=0, keepdims=True
    )
    place_of = (
        (block_of - begin) * SLOTS
        + chunk * rows
        + lax.broadcasted_iota(i32, (1, rows), 1)
        - first_row
    )
    select = jnp.where(
        lax.broadcasted_iota(i32, (window * SLOTS, rows), 0) == place_of, 1.0, 0.0
    ).astype(bf16)

    slope = gelu_slope(hidden_ref[...].astype(f32))
    greeted = (
        jnp.where(first + 1 < chunks, jnp.where(start_of(first + 1) <= loop, 1, 0), 0)
        + jnp.where(first + 2 < chunks, jnp.where(start_of(first + 2) <= loop, 1, 0), 0)
        + 1
    )
    own_window = (
        (slice_home == chunk) & (begin <= loop) & (loop < begin + window)
    )
    pl.semaphore_wait(
        barrier,
        greeted * (experts * halves) + window + (ring - 1) + 2 - jnp.where(own_window, 2, 0),
    )

    def a_copy(e, k, h, l, t):
        return pltpu.make_async_remote_copy(
            src_ref=slot_ref.at[e, h, used],
            dst_ref=arrive_ref.at[loop - start_of(t), used],
            send_sem=a_send.at[e, k, h],
            recv_sem=a_recv,
            device_id=(l, t),
            device_id_type=MESH,
        )

    def a_start(e, k, h, l, t):
        @pl.when((l != loop) | (t != chunk))
        def _():
            a_copy(e, k, h, l, t).start()

        @pl.when((l == loop) & (t == chunk))
        def _():
            pltpu.make_async_copy(
                slot_ref.at[e, h, used], arrive_ref.at[loop - start_of(t), used], a_recv
            ).start()

    def a_finish(e, k, h, l, t):
        @pl.when((l != loop) | (t != chunk))
        def _():
            a_copy(e, k, h, l, t).wait_send()

    targets(a_start)

    for c in range(CORES):
        for p in range(PLANES):
            for s in range(ring):
                t = home_of(expert, chunk, p, s)
                source = pl.ds(pl.multiple_of((t * CORES + c) * piece, piece), piece)
                target = pl.ds((c * (PLANES * ring) + p * ring + s) * piece, piece)
                pltpu.make_async_copy(
                    out_hbm.at[:, source], out_ref.at[:, target], weight_sem.at[0]
                ).start()
                pltpu.make_async_copy(
                    in_hbm.at[source, :], in_ref.at[target, :], weight_sem.at[1]
                ).start()
    weights = (
        pltpu.make_async_copy(out_ref, out_ref, weight_sem.at[0]),
        pltpu.make_async_copy(in_ref, in_ref, weight_sem.at[1]),
    )
    everything = arrive_ref.at[:, used]
    pltpu.make_async_copy(everything, everything, a_recv).wait()
    mine = dot_tn(select, arrive_ref[...].reshape(window * SLOTS, piece)).astype(bf16)
    wide_ref[:, at_slice(core, plane, spot)] = mine

    order = by_distance(ring)

    def bx_copy(d):
        here = wide_ref.at[:, at_slice(core, plane, spot)]
        return pltpu.make_async_remote_copy(
            src_ref=here,
            dst_ref=here,
            send_sem=bx_send.at[d],
            recv_sem=bx_recv.at[d],
            device_id=(loop_of(expert, plane, lax.rem(spot + d, ring), core), chunk),
            device_id_type=MESH,
        )

    beside = (1, ring - 1) if ring > 2 else ()

    def bz_copy(d):
        if d in beside:
            here = wide_ref.at[:, at_slice(core, 1 - plane, spot)]
            target = loop_of(expert, plane, lax.rem(spot + d, ring), core)
        else:
            here = wide_ref.at[:, at_slice(core, plane, lax.rem(spot + ring - d, ring))]
            target = loop_of(expert, 1 - plane, spot, core)
        return pltpu.make_async_remote_copy(
            src_ref=here,
            dst_ref=here,
            send_sem=bz_send.at[d],
            recv_sem=bz_recv.at[d],
            device_id=(target, chunk),
            device_id_type=MESH,
        )

    def bc_copy(p, d):
        other = plane if p == 0 else 1 - plane
        here = wide_ref.at[:, at_slice(core, other, lax.rem(spot + ring - d, ring))]
        return pltpu.make_async_remote_copy(
            src_ref=here,
            dst_ref=here,
            send_sem=bc_send.at[p, d],
            recv_sem=bc_recv.at[p, d],
            device_id=(loop_of(expert, plane, spot, 1 - core), chunk),
            device_id_type=MESH,
        )

    def quarter_of(c, p):
        return pl.ds(pl.multiple_of((c * PLANES + p) * quarter, quarter), quarter)

    def first_product(c, p):
        here = quarter_of(c, p)
        return dot_nt(wide_ref[:, here], out_ref[:, here])

    for d in order:
        bx_copy(d).start()
    bz_copy(0).start()
    bc_copy(0, 0).start()
    for i, d in enumerate(order):
        bx_copy(d).wait_recv()
        if i == min(1, len(order) - 1):
            bz_copy(0).wait_recv()
            for n in beside:
                bz_copy(n).start()
            bc_copy(1, 0).start()
        if d not in beside:
            bz_copy(d).start()
        bc_copy(0, d).start()
    weights[0].wait()
    act = first_product(core, plane)
    for d in [0] + order:
        bc_copy(0, d).wait_recv()
    act += first_product(1 - core, plane)
    if not order:
        bz_copy(0).wait_recv()
        bc_copy(1, 0).start()
    for d in order:
        bz_copy(d).wait_recv()
        bc_copy(1, d).start()
    act += first_product(core, 1 - plane)
    for d in [0] + order:
        bc_copy(1, d).wait_recv()
    act += first_product(1 - core, 1 - plane)
    pre = (act * slope).astype(bf16)

    def second_product(c, p):
        return dot_nt(pre, in_ref[quarter_of(c, p), :])

    def cc_copy(p):
        return pltpu.make_async_remote_copy(
            src_ref=core_send.at[p],
            dst_ref=core_recv.at[p],
            send_sem=cc_send.at[p],
            recv_sem=cc_recv.at[p],
            device_id=(loop_of(expert, plane, spot, 1 - core), chunk),
            device_id_type=MESH,
        )

    def at_spot(s):
        return pl.ds(pl.multiple_of(s * piece, piece), piece)

    def cz_copy(d):
        here = at_spot(lax.rem(spot + d, ring))
        return pltpu.make_async_remote_copy(
            src_ref=plane_send.at[:, here] if d else last_send,
            dst_ref=plane_recv.at[:, here],
            send_sem=cz_send.at[d],
            recv_sem=cz_recv.at[d],
            device_id=(loop_of(expert, 1 - plane, spot, core), chunk),
            device_id_type=MESH,
        )

    def cx_copy(d):
        return pltpu.make_async_remote_copy(
            src_ref=ring_send.at[d],
            dst_ref=ring_recv.at[d],
            send_sem=cx_send.at[d],
            recv_sem=cx_recv.at[d],
            device_id=(loop_of(expert, plane, lax.rem(spot + d, ring), core), chunk),
            device_id_type=MESH,
        )

    def side_copy(d):
        return pltpu.make_async_remote_copy(
            src_ref=plane_send.at[:, at_spot(lax.rem(spot + d, ring))],
            dst_ref=side_recv.at[beside.index(d)],
            send_sem=cs_send.at[beside.index(d)],
            recv_sem=cs_recv.at[beside.index(d)],
            device_id=(loop_of(expert, plane, lax.rem(spot + d, ring), core), chunk),
            device_id_type=MESH,
        )

    far_first = [d for d in reversed(order) if d not in beside]
    weights[1].wait()
    core_send[1] = second_product(1 - core, 1 - plane).astype(core_send.dtype)
    cc_copy(1).start()
    core_send[0] = second_product(1 - core, plane).astype(core_send.dtype)
    cc_copy(0).start()
    partial = second_product(core, 1 - plane)
    cc_copy(1).wait_recv()
    own_ref[...] = partial + core_recv[1].astype(f32)
    plane_send[...] = own_ref[...].astype(bf16)
    for d in far_first + list(beside):
        (side_copy if d in beside else cz_copy)(d).start()
    here_sum = own_ref[:, at_spot(spot)]
    partial = second_product(core, plane)
    cc_copy(0).wait_recv()
    own_ref[...] = partial + core_recv[0].astype(f32)
    for d in beside:
        ring_send[d] = own_ref[:, at_spot(lax.rem(spot + d, ring))].astype(bf16)
        cx_copy(d).start()
    for d in beside:
        side_copy(d).wait_recv()
        here_sum += side_recv[beside.index(d)].astype(f32)
    last_send[...] = here_sum.astype(bf16)
    cz_copy(0).start()
    for d in far_first:
        cz_copy(d).wait_recv()
        here = at_spot(lax.rem(spot + d, ring))
        ring_send[d] = (own_ref[:, here] + plane_recv[:, here].astype(f32)).astype(bf16)
        cx_copy(d).start()
    cz_copy(0).wait_recv()
    total = own_ref[:, at_spot(spot)] + plane_recv[:, at_spot(spot)].astype(f32)
    for d in order:
        cx_copy(d).wait_recv()
        total += ring_recv[d].astype(f32)

    back = dot_nn(select, total.astype(bf16)).astype(bf16)
    back_ref[...] = back.reshape(window, SLOTS, piece)

    def d_copy(i):
        home = begin + i
        k = chunk - first_of(home)
        return pltpu.make_async_remote_copy(
            src_ref=back_ref.at[i, used],
            dst_ref=home_ref.at[expert, k, slice_half, used],
            send_sem=d_send.at[i],
            recv_sem=d_recv.at[expert, k, slice_half],
            device_id=(home, slice_home),
            device_id_type=MESH,
        )

    def d_start(i):
        home = begin + i

        @pl.when((home != loop) | (slice_home != chunk))
        def _():
            d_copy(i).start()

        @pl.when((home == loop) & (slice_home == chunk))
        def _():
            k = chunk - first_of(home)
            pltpu.make_async_copy(
                back_ref.at[i, used],
                home_ref.at[expert, k, slice_half, used],
                d_recv.at[expert, k, slice_half],
            ).start()

    for i in range(window):
        d_start(i)

    targets(a_finish)
    for d in order:
        bx_copy(d).wait_send()
        cx_copy(d).wait_send()
    for d in [0] + order:
        bz_copy(d).wait_send()
        (side_copy if d in beside else cz_copy)(d).wait_send()
        for p in range(PLANES):
            bc_copy(p, d).wait_send()
    for p in range(PLANES):
        cc_copy(p).wait_send()

    def d_wait(e, k, h, l, t):
        pltpu.make_async_copy(
            home_ref.at[e, k, h, used], home_ref.at[e, k, h, used], d_recv.at[e, k, h]
        ).wait()

    targets(d_wait)
    moe = jnp.zeros((block_rows, home_cols), f32)
    for e in range(experts):
        parts = []
        for h in range(halves):
            part = home_ref[e, 0, h].astype(f32)
            for k in range(1, CHUNKS):
                part += home_ref[e, k, h].astype(f32)
            parts.append(part)
        moe += dot_nn(spread[e], jnp.concatenate(parts, axis=1).astype(bf16))
    result_ref[...] = (grad_ref[...].astype(f32) + moe).astype(result_ref.dtype)
    for i in range(window):
        home = begin + i

        @pl.when((home != loop) | (slice_home != chunk))
        def _():
            d_copy(i).wait_send()


def shards(ring, grad_out, saved_hidden, picked_tokens, gate_values, in_weight, out_weight):
    blocks, chunks = lax.axis_size("loop"), lax.axis_size("tensor")
    experts, capacity = picked_tokens.shape
    rows, width = saved_hidden.shape[0], in_weight.shape[1]
    features = in_weight.shape[0]
    window = window_size(blocks, capacity, chunks)
    group = blocks // experts
    piece = features // group
    halves = group // chunks
    quarter = features // (CORES * PLANES)
    bf16, f32 = jnp.bfloat16, jnp.float32
    vmem, dma = pltpu.VMEM, pltpu.SemaphoreType.DMA
    in_vmem = pl.BlockSpec(memory_space=pltpu.VMEM)
    in_hbm = pl.BlockSpec(memory_space=pl.ANY)
    return pl.pallas_call(
        functools.partial(kernel, (experts, chunks, blocks, ring, window)),
        out_shape=pltpu.VMEM(grad_out.shape, bf16),
        in_specs=[in_hbm] * 6,
        out_specs=in_vmem,
        scratch_shapes=[
            vmem(grad_out.shape, bf16),
            vmem(saved_hidden.shape, bf16),
            vmem(picked_tokens.shape, jnp.int32),
            vmem(gate_values.shape, f32),
            vmem((features, width), bf16),
            vmem((width, features), bf16),
            vmem((experts, halves, SLOTS, piece), bf16),
            vmem((window, SLOTS, piece), bf16),
            vmem((rows, features), bf16),
            vmem((PLANES, rows, quarter), bf16),
            vmem((PLANES, rows, quarter), bf16),
            vmem((rows, quarter), bf16),
            vmem((rows, quarter), bf16),
            vmem((rows, quarter), f32),
            vmem((2, rows, piece), bf16),
            vmem((rows, piece), bf16),
            vmem((ring, rows, piece), bf16),
            vmem((ring, rows, piece), bf16),
            vmem((window, SLOTS, piece), bf16),
            vmem((experts, CHUNKS, halves, SLOTS, piece), bf16),
            dma((4,)),
            dma((2,)),
            dma((experts, CHUNKS, halves)),
            dma,
            dma((ring,)),
            dma((ring,)),
            dma((ring,)),
            dma((ring,)),
            dma((PLANES, ring)),
            dma((PLANES, ring)),
            dma((PLANES,)),
            dma((PLANES,)),
            dma((ring,)),
            dma((ring,)),
            dma((ring,)),
            dma((ring,)),
            dma((2,)),
            dma((2,)),
            dma((window,)),
            dma((experts, CHUNKS, halves)),
        ],
        compiler_params=pltpu.CompilerParams(collective_id=0, has_side_effects=True),
    )(
        grad_out,
        saved_hidden,
        picked_tokens,
        gate_values,
        in_weight,
        out_weight,
    )


def solution(mesh):
    ring = mesh.shape["loop"] // (2 * PLANES * CORES)
    placed = (
        P("loop", "tensor"),
        P("tensor", "loop"),
        P(),
        P(),
        P(None, "loop"),
        P("loop", None),
    )
    return jax.shard_map(
        functools.partial(shards, ring),
        mesh=mesh,
        in_specs=placed,
        out_specs=P("loop", "tensor"),
        check_vma=False,
    )
```
